32 devices in a mesh: tok: 8 (over y, x, core), head: 4 (over z).
Axes of the slice: x: 2, y: 2, z: 4, core: 2. Of those that a mesh axis runs over, the one named last changes fastest.
Arguments:
- layer_input: bfloat16 [4096, 5120], P('tok', 'head'), may hold values from -6 to 6
- rate_weight: bfloat16 [5120, 12], P('head'), may hold values from -0.078125 to 0.078125
- token_queries: bfloat16 [4096, 3072], P('tok', 'head'), may hold values from -80 to 80
- token_keys: bfloat16 [4096, 3072], P('tok', 'head'), may hold values from -5 to 5
- token_values: bfloat16 [4096, 3072], P('tok', 'head'), may hold values from -6 to 6
- first_weight: float32 [12, 256, 512], P('head'), may hold values from -0.375 to 0.375
- third_weight: float32 [12, 256, 512], P('head'), may hold values from -0.375 to 0.375
- second_weight: float32 [12, 512, 256], P('head'), may hold values from -0.25 to 0.25
- update_scale: float32 [12], P('head'), may hold values from 0.5 to 2
- out_gain: float32 [3072], P('head'), may hold values from 0.25 to 1.75
Outputs:
- mixed: bfloat16 [4096, 3072], P('tok', 'head')
The draws below stay inside these ranges and needn't reach their ends.
All inputs are finite; a program needn't handle non-finite values.
Results may differ from the reference program's by a relative error of at most 0.033.
Values may be sent and summed in bfloat16 or wider, within the bound.
No kernel may reach another device: no remote copies, remote signals or barrier semaphores. Data moves between devices by JAX's collectives and lax.ppermute only.
A program may use at most 128 MiB of HBM per device.

```python
import math
import jax
import jax.numpy as jnp
from jax import lax

D = 5120
HEADS = 12
HDIM = 256
FFN = 512
WINDOW = 256
STEPS = 5
TOKENS = 4096


def query_key_pair(key):
    base = jax.random.fold_in(key, 7311)
    first, second = jax.random.split(base, 2)
    shape = (TOKENS, HEADS * HDIM)
    drawn_keys = jnp.clip(jax.random.normal(first, shape, jnp.float32), -4.5, 4.5)
    drawn_queries = jnp.clip(jax.random.normal(second, shape, jnp.float32), -4.5, 4.5)
    return (drawn_queries, drawn_keys)


def draw_token_queries(key, part):
    return query_key_pair(key)[0].astype(jnp.bfloat16)


def draw_token_keys(key, part):
    return query_key_pair(key)[1].astype(jnp.bfloat16)


def block_scale(stream_key, dims, cuts, smallest, largest):
    factor_of = 1.0
    for axis_at, shards_of in cuts:
        draws = jax.random.uniform(jax.random.fold_in(jax.random.fold_in(stream_key, 6), axis_at), (shards_of,), jnp.float32, smallest / len(cuts), largest / len(cuts))
        factor_of = factor_of * jnp.repeat(jnp.exp(draws), dims[axis_at] // shards_of).reshape((-1,) + (1,) * (len(dims) - 1 - axis_at))
    return factor_of


def normal_values(stream_key, dims, width, most, pieces=(), held_as=jnp.bfloat16):
    values = width * jax.random.normal(stream_key, dims, jnp.float32)
    if pieces:
        values = values * block_scale(stream_key, dims, pieces, -0.22, 0.18)
    return jnp.clip(values, -most, most).astype(held_as)


def setup_inputs(seed: int = 0) -> dict:
    streams_of = jax.random.split(jax.random.key(seed), 11)
    layer_input = normal_values(streams_of[0], (TOKENS, D), 1.0, 6.0, ((0, 8), (1, 4)))
    rate_weight = normal_values(streams_of[1], (D, HEADS), D ** -0.5, 0.078125, ((0, 4),))
    token_queries = draw_token_queries(jax.random.fold_in(streams_of[10], 71), 0)
    token_keys = draw_token_keys(jax.random.fold_in(streams_of[10], 71), 0)
    token_values = normal_values(streams_of[4], (TOKENS, HEADS * HDIM), 1.0, 6.0, ((0, 8), (1, 4)))
    first_weight = normal_values(streams_of[5], (HEADS, HDIM, FFN), HDIM ** -0.5, 0.375, ((0, 4),), jnp.float32)
    third_weight = normal_values(streams_of[6], (HEADS, HDIM, FFN), HDIM ** -0.5, 0.375, ((0, 4),), jnp.float32)
    second_weight = normal_values(streams_of[7], (HEADS, FFN, HDIM), FFN ** -0.5, 0.25, ((0, 4),), jnp.float32)
    update_scale = jnp.clip(jnp.exp(math.log(2.0) - 1.3862944 * jax.random.uniform(streams_of[8], (HEADS,), jnp.float32) ** block_scale(streams_of[8], (HEADS,), ((0, 4),), -0.2, 0.2)), 0.5, 2.0)
    out_gain = jnp.clip(1.0 + 0.15 * jax.random.normal(streams_of[9], (HEADS * HDIM,), jnp.float32), 0.25, 1.75)
    return {"layer_input": layer_input, "rate_weight": rate_weight, "token_queries": token_queries, "token_keys": token_keys, "token_values": token_values, "first_weight": first_weight, "third_weight": third_weight, "second_weight": second_weight, "update_scale": update_scale, "out_gain": out_gain}


COEF_A = 3.4445
COEF_B = -4.775
COEF_C = 2.0315
EPS_SCALE = 1e-07
EPS_RMS = 1e-06

def fast_gradient(inputs):
    key_head, value_head, rate_head, first_head, third_head, second_head = inputs
    first_half = first_head.astype(jnp.bfloat16)
    third_half = third_head.astype(jnp.bfloat16)
    second_half = second_head.astype(jnp.bfloat16)
    gate_pre = jnp.dot(key_head, first_half, preferred_element_type=jnp.float32)
    up_pre = jnp.dot(key_head, third_half, preferred_element_type=jnp.float32)
    sigmoid_gate = jax.nn.sigmoid(gate_pre)
    activated = gate_pre * sigmoid_gate
    hidden = (activated * up_pre).astype(jnp.bfloat16)
    weighted = (value_head.astype(jnp.float32) * rate_head[:, None]).astype(jnp.bfloat16)
    hidden_grad = -jnp.dot(weighted, second_half.T, preferred_element_type=jnp.float32)
    gate_grad = (hidden_grad * up_pre * sigmoid_gate * (1.0 + gate_pre * (1.0 - sigmoid_gate))).astype(jnp.bfloat16)
    up_grad = (hidden_grad * activated).astype(jnp.bfloat16)
    first_grad = jnp.dot(key_head.T, gate_grad, preferred_element_type=jnp.float32)
    third_grad = jnp.dot(key_head.T, up_grad, preferred_element_type=jnp.float32)
    second_grad = -jnp.dot(weighted.T, hidden, preferred_element_type=jnp.float32)
    return (first_grad, third_grad, second_grad)

def orthogonalize(stacked):
    scale = jnp.sqrt(lax.optimization_barrier(jnp.sum(stacked * stacked, axis=(1, 2))))
    iterate = (stacked / (scale[:, None, None] + EPS_SCALE)).astype(jnp.bfloat16)
    for repeat in range(STEPS):
        wide = iterate.astype(jnp.float32)
        gram_half = jnp.einsum('mik,mjk->mij', wide, wide, precision=lax.Precision.HIGHEST).astype(jnp.bfloat16)
        gram_wide = gram_half.astype(jnp.float32)
        squared = jnp.einsum('mij,mjk->mik', gram_wide, gram_wide, precision=lax.Precision.HIGHEST)
        mixing = (COEF_B * gram_wide + COEF_C * squared).astype(jnp.bfloat16)
        moved = jnp.einsum('mij,mjk->mik', mixing.astype(jnp.float32), wide, precision=lax.Precision.HIGHEST)
        iterate = (COEF_A * wide + moved).astype(jnp.bfloat16)
    return iterate

def fast_apply(query_head, first_head, third_head, second_head, gain_head):
    gate_pre = jnp.dot(query_head, first_head.astype(jnp.bfloat16), preferred_element_type=jnp.float32)
    up_pre = jnp.dot(query_head, third_head.astype(jnp.bfloat16), preferred_element_type=jnp.float32)
    hidden = (gate_pre * jax.nn.sigmoid(gate_pre) * up_pre).astype(jnp.bfloat16)
    output = jnp.dot(hidden, second_head.astype(jnp.bfloat16), preferred_element_type=jnp.float32)
    return output * lax.rsqrt(lax.optimization_barrier(jnp.mean(output * output, axis=-1, keepdims=True)) + EPS_RMS) * gain_head

def window_attention(query_head, key_head, value_head):
    block_rows = min(512, TOKENS)
    padded_keys = jnp.concatenate([jnp.zeros((WINDOW, HDIM), key_head.dtype), key_head])
    padded_values = jnp.concatenate([jnp.zeros((WINDOW, HDIM), value_head.dtype), value_head])
    starts = jnp.arange(TOKENS // block_rows, dtype=jnp.int32) * block_rows

    def one_block(start):
        query_block = lax.dynamic_slice_in_dim(query_head, start, block_rows, 0)
        key_block = lax.dynamic_slice_in_dim(padded_keys, start, block_rows + WINDOW, 0)
        value_block = lax.dynamic_slice_in_dim(padded_values, start, block_rows + WINDOW, 0)
        query_place = start + jnp.arange(block_rows, dtype=jnp.int32)
        key_place = start - WINDOW + jnp.arange(block_rows + WINDOW, dtype=jnp.int32)
        scores = jnp.dot(query_block, key_block.T, preferred_element_type=jnp.float32) * HDIM ** (-0.5)
        allowed = (key_place[None, :] <= query_place[:, None]) & (key_place[None, :] > query_place[:, None] - WINDOW) & (key_place[None, :] >= 0)
        scores = jnp.where(allowed, scores, -1e+30)
        highest = lax.optimization_barrier(jnp.max(scores, axis=-1, keepdims=True))
        weights = jnp.exp(scores - highest)
        shares = (weights / lax.optimization_barrier(jnp.sum(weights, axis=-1, keepdims=True))).astype(jnp.bfloat16)
        return jnp.dot(shares, value_block, preferred_element_type=jnp.float32)
    return lax.map(one_block, starts).reshape(TOKENS, HDIM)

def reference(layer_input, rate_weight, token_queries, token_keys, token_values, first_weight, third_weight, second_weight, update_scale, out_gain):
    token_rates = jax.nn.softplus(jnp.dot(layer_input, rate_weight, preferred_element_type=jnp.float32))

    def by_head(array):
        return array.reshape(TOKENS, HEADS, HDIM).transpose(1, 0, 2)
    query_heads = by_head(token_queries)
    key_heads = by_head(token_keys)
    value_heads = by_head(token_values)
    first_grad, third_grad, second_grad = lax.map(fast_gradient, (key_heads, value_heads, token_rates.T, first_weight, third_weight, second_weight))
    stacked = jnp.concatenate([first_grad, third_grad, second_grad], axis=0)
    ortho = orthogonalize(stacked).astype(jnp.float32)
    step_size = update_scale[:, None, None]
    new_first = first_weight - step_size * ortho[:HEADS]
    new_third = third_weight - step_size * ortho[HEADS:2 * HEADS]
    new_second = second_weight - step_size * jnp.swapaxes(ortho[2 * HEADS:], 1, 2)
    gains = out_gain.reshape(HEADS, HDIM)

    def head_output(inputs):
        query_head, key_head, value_head, first_head, third_head, second_head, gain_head = inputs
        normed = fast_apply(query_head, first_head, third_head, second_head, gain_head)
        return normed + window_attention(query_head, key_head, value_head)
    outputs = lax.map(head_output, (query_heads, key_heads, value_heads, new_first, new_third, new_second, gains))
    return outputs.transpose(1, 0, 2).reshape(TOKENS, HEADS * HDIM).astype(jnp.bfloat16)
```

```python
import functools

import jax
import jax.numpy as jnp
from jax import lax
from jax.experimental import pallas as pl
from jax.experimental.pallas import tpu as pltpu
from jax.sharding import PartitionSpec as P

HDIM = 256
WINDOW = 256
STEPS = 5
KINDS = 3


COEF_A = 3.4445
COEF_B = -4.775
COEF_C = 2.0315
EPS_SCALE = 1e-07
EPS_RMS = 1e-06

SUBLANES = 8
NT = (((1,), (1,)), ((), ()))


VMEM_LIMIT = 60 * 1024 * 1024


def matmul(a, b):
    return jnp.dot(a, b, preferred_element_type=jnp.float32)


def matmul_nt(a, b):
    return lax.dot_general(a, b, NT, preferred_element_type=jnp.float32)


def exchanged(block, axis, distance):
    route = [(i, i ^ distance) for i in range(lax.axis_size(axis))]
    return lax.ppermute(block, axis, route)


def passed_along(block, axis):
    count = lax.axis_size(axis)
    return lax.ppermute(block, axis, [(i, i + 1) for i in range(count - 1)])


def call(kernel, outs, *args, name, scalars=(), grid=None, in_specs=None, out_specs=None,
         scratch=(), flops=0, moved=0):
    extra = {}
    if grid is None:
        grid = (1,)
    if in_specs is None:
        in_specs = [whole(a.shape) for a in args]
    if out_specs is None:
        out_specs = [whole(o.shape) for o in outs]
    spec = pltpu.PrefetchScalarGridSpec(
        num_scalar_prefetch=len(scalars),
        grid=grid,
        in_specs=in_specs,
        out_specs=out_specs,
        scratch_shapes=list(scratch),
    )
    return pl.pallas_call(
        kernel,
        out_shape=list(outs),
        grid_spec=spec,
        name=name,
        compiler_params=pltpu.CompilerParams(vmem_limit_bytes=VMEM_LIMIT),
        cost_estimate=pl.CostEstimate(flops=flops, bytes_accessed=moved, transcendentals=0),
        **extra,
    )(*scalars, *args)


def whole(shape):
    return pl.BlockSpec(shape, lambda *_: (0,) * len(shape))


def struct(shape, dtype):
    return jax.ShapeDtypeStruct(shape, dtype)


def sigmoid(x):
    return 1.0 / (1.0 + jnp.exp(-x))


def logits_kernel(where, x_ref, w_ref, k_ref, v_ref, keep_ref, send_ref, tail_ref, *, local_heads):
    logits = matmul(x_ref[...], w_ref[...]).T
    bit = where[1] % 2
    keep_ref[...] = jnp.zeros_like(keep_ref)
    send_ref[...] = jnp.zeros_like(send_ref)
    for pair in range(keep_ref.shape[0]):
        first = logits[2 * pair * local_heads : (2 * pair + 1) * local_heads]
        second = logits[(2 * pair + 1) * local_heads : (2 * pair + 2) * local_heads]
        keep_ref[pair, 0:local_heads, :] = jnp.where(bit == 0, first, second)
        send_ref[pair, 0:local_heads, :] = jnp.where(bit == 0, second, first)
    rows = k_ref.shape[0]
    tail_ref[0:rows, :] = k_ref[...]
    tail_ref[rows : 2 * rows, :] = v_ref[...]


def backward_kernel(k_ref, v_ref, w1_ref, w3_ref, w2_ref, grads_ref, hidden_ref, kt_ref, vt_ref):
    ffn = w1_ref.shape[2]
    keys = k_ref[...]
    values = v_ref[...]
    w1 = w1_ref[0].astype(jnp.bfloat16)
    w3 = w3_ref[0].astype(jnp.bfloat16)
    w2 = w2_ref[0].astype(jnp.bfloat16)
    rows = keys.shape[0]
    step = min(128, rows)
    for at in range(0, rows, step):
        block = slice(at, at + step)
        gate = matmul(keys[block], w1)
        upper = matmul(keys[block], w3)
        back = -matmul_nt(values[block], w2)
        sig = sigmoid(gate)
        activ = gate * sig
        hidden_ref[block, :] = (activ * upper).astype(jnp.bfloat16)
        grads_ref[block, 0:ffn] = (back * upper * sig * (1.0 + gate * (1.0 - sig))).astype(
            jnp.bfloat16
        )
        grads_ref[block, ffn : 2 * ffn] = (back * activ).astype(jnp.bfloat16)
    kt_ref[...] = keys.T
    vt_ref[...] = values.T


def gradient_kernel(where, keep_logit_ref, got_logit_ref, *refs, local_heads, owners):
    ins, (keep_ref, send_ref) = refs[:-2], refs[-2:]
    rates = jax.nn.softplus(keep_logit_ref[...] + got_logit_ref[...])
    core = where[0] % 2
    shared_at = (owners // 2) * HDIM

    def put(index, value):
        if index < owners:
            rows = slice((index // 2) * HDIM, (index // 2 + 1) * HDIM)

            @pl.when(core == index % 2)
            def _():
                keep_ref[rows, :] = value

            @pl.when(core != index % 2)
            def _():
                send_ref[rows, :] = value.astype(jnp.bfloat16)
        else:
            half = HDIM // 2
            at = shared_at + (index - owners) * half
            for side in range(2):
                part = value[side * half : (side + 1) * half]

                @pl.when(core == side)
                def _():
                    keep_ref[at : at + half, :] = part

                @pl.when(core != side)
                def _():
                    send_ref[at : at + half, :] = part.astype(jnp.bfloat16)

    for head in range(local_heads):
        grads_ref, hidden_ref, kt_ref, vt_ref = ins[4 * head : 4 * head + 4]
        ffn = hidden_ref.shape[1]
        rate = rates[head : head + 1]
        keys = (kt_ref[...].astype(jnp.float32) * rate).astype(jnp.bfloat16)
        values = (vt_ref[...].astype(jnp.float32) * rate).astype(jnp.bfloat16)
        put(KINDS * head, matmul(keys, grads_ref[:, 0:ffn]))
        put(KINDS * head + 1, matmul(keys, grads_ref[:, ffn : 2 * ffn]))
        put(KINDS * head + 2, -matmul(values, hidden_ref[...]))


def chip_sum_kernel(where, keep_ref, got_ref, own_ref, *send_refs, owners, shared):
    chips = owners // 2
    chip = (where[0] // 2) % chips
    part = HDIM // owners
    for relative in range(chips):
        other = chip ^ relative
        out = own_ref if relative == 0 else send_refs[relative - 1]
        rows = pl.ds(pl.multiple_of(other * HDIM, HDIM), HDIM)
        out[0:HDIM, :] = (keep_ref[rows, :] + got_ref[rows, :].astype(jnp.float32)).astype(
            out.dtype
        )
        for extra in range(shared):
            start = chips * HDIM + extra * (HDIM // 2)
            rows = pl.ds(pl.multiple_of(start + other * part, part), part)
            at = HDIM + extra * part
            out[at : at + part, :] = (
                keep_ref[rows, :] + got_ref[rows, :].astype(jnp.float32)
            ).astype(out.dtype)


def weight_kernel(where, w1_ref, w3_ref, w2_ref, last_ref, own_ref, shared_ref, *, owners):
    kind = (where[0] % owners) % KINDS

    @pl.when(kind == 0)
    def _():
        own_ref[...] = w1_ref[0]

    @pl.when(kind == 1)
    def _():
        own_ref[...] = w3_ref[0]

    @pl.when(kind == 2)
    def _():
        own_ref[...] = w2_ref[0].T

    shared_ref[...] = last_ref[0].T


def normalized(total):
    size = jnp.sqrt(jnp.sum(total * total, keepdims=True)) + EPS_SCALE
    return (total * (1.0 / size)).astype(jnp.bfloat16)


def polish(iterate):
    gram = matmul_nt(iterate, iterate).astype(jnp.bfloat16)
    squared = matmul(gram, gram)
    mixing = (COEF_B * gram.astype(jnp.float32) + COEF_C * squared).astype(jnp.bfloat16)
    return (COEF_A * iterate.astype(jnp.float32) + matmul(mixing, iterate)).astype(jnp.bfloat16)


def update_kernel(where, scale_ref, weight_ref, *refs, owners):
    addends, out_ref = refs[:-1], refs[-1]
    total = addends[0][...]
    for ref in addends[1:]:
        total = total + ref[...].astype(jnp.float32)
    iterate = normalized(total[0:HDIM])
    out_ref[HDIM:, :] = total[HDIM:].astype(jnp.bfloat16)
    for _ in range(STEPS):
        iterate = polish(iterate)
    scale = scale_ref[(where[0] % owners) // KINDS]
    out_ref[0:HDIM, :] = (weight_ref[...] - scale * iterate.astype(jnp.float32)).astype(
        jnp.bfloat16
    )


def attention_kernel(where, q_ref, k_ref, v_ref, pk_ref, pv_ref, out_ref):
    rows = q_ref.shape[0]
    query_at = lax.broadcasted_iota(jnp.int32, (WINDOW, WINDOW), 0)
    key_at = lax.broadcasted_iota(jnp.int32, (WINDOW, WINDOW), 1)
    causal = key_at <= query_at
    inside = key_at > query_at
    for block in range(rows // WINDOW):
        here = slice(block * WINDOW, (block + 1) * WINDOW)
        before = slice((block - 1) * WINDOW, block * WINDOW)
        query = q_ref[here, :]
        if block == 0:
            left_key, left_value = pk_ref[...], pv_ref[...]
            left_mask = inside & (where[0] > 0)
        else:
            left_key, left_value = k_ref[before, :], v_ref[before, :]
            left_mask = inside
        left = jnp.where(left_mask, matmul_nt(query, left_key) * HDIM ** (-0.5), -1e30)
        right = jnp.where(causal, matmul_nt(query, k_ref[here, :]) * HDIM ** (-0.5), -1e30)
        highest = jnp.maximum(
            jnp.max(left, axis=-1, keepdims=True), jnp.max(right, axis=-1, keepdims=True)
        )
        left = jnp.exp(left - highest)
        right = jnp.exp(right - highest)
        inverse = 1.0 / (
            jnp.sum(left, axis=-1, keepdims=True) + jnp.sum(right, axis=-1, keepdims=True)
        )
        out_ref[here, :] = matmul((left * inverse).astype(jnp.bfloat16), left_value) + matmul(
            (right * inverse).astype(jnp.bfloat16), v_ref[here, :]
        )


def apply_kernel(where, scale_ref, q_ref, attended_ref, gain_ref, weight_ref, *refs,
                 local_heads, owners, shared):
    parts, (out_ref, held_ref, total_ref) = refs[:-3], refs[-3:]
    chips = owners // 2
    part = HDIM // owners
    chip = (where[0] // 2) % chips
    core = where[0] % 2
    for relative in range(chips):
        for side in range(2):
            ref = parts[relative + side * chips]
            from_chip = chip ^ relative
            from_core = core ^ side
            held_ref[from_chip * 2 + from_core] = ref[0:HDIM, :]
            for extra in range(shared):
                at = from_core * (HDIM // 2) + from_chip * part
                total_ref[extra, pl.ds(pl.multiple_of(at, part), part), :] = ref[
                    HDIM + extra * part : HDIM + (extra + 1) * part, :
                ]
    for extra in range(shared):
        iterate = normalized(total_ref[extra].astype(jnp.float32))
        for _ in range(STEPS):
            iterate = polish(iterate)
        scale = scale_ref[(owners + extra) // KINDS]
        held_ref[owners + extra] = (
            weight_ref[...] - scale * iterate.astype(jnp.float32)
        ).astype(jnp.bfloat16)
    rows = q_ref.shape[0]
    step = min(256, rows)
    for head in range(local_heads):
        columns = slice(head * HDIM, (head + 1) * HDIM)
        for at in range(0, rows, step):
            block = slice(at, at + step)
            query = q_ref[block, columns]
            gate = matmul(query, held_ref[KINDS * head])
            upper = matmul(query, held_ref[KINDS * head + 1])
            hidden = (gate * sigmoid(gate) * upper).astype(jnp.bfloat16)
            out = matmul_nt(hidden, held_ref[KINDS * head + 2])
            mean = jnp.mean(out * out, axis=-1, keepdims=True)
            normed = out * lax.rsqrt(mean + EPS_RMS) * gain_ref[:, columns]
            out_ref[block, columns] = (normed + attended_ref[block, columns]).astype(
                jnp.bfloat16
            )


def on_device(
    layer_input,
    rate_weight,
    token_queries,
    token_keys,
    token_values,
    first_weight,
    third_weight,
    second_weight,
    update_scale,
    out_gain,
):
    rows, width = token_queries.shape
    local_heads = width // HDIM
    ffn = first_weight.shape[2]
    tok_count = lax.axis_size("tok")
    head_count = lax.axis_size("head")
    matrices = KINDS * local_heads
    owners = 1
    while owners * 2 <= min(tok_count, matrices):
        owners *= 2
    shared = matrices - owners
    chips = owners // 2
    part = HDIM // owners
    where = jnp.stack([lax.axis_index("tok"), lax.axis_index("head")]).astype(jnp.int32)
    f32, bf16 = jnp.float32, jnp.bfloat16

    features = layer_input.shape[1]
    slab = struct((head_count // 2, SUBLANES, rows), f32)
    tail_at = rows // WINDOW - 1
    keep, send, tail = call(
        functools.partial(logits_kernel, local_heads=local_heads),
        [slab, slab, struct((2 * WINDOW, width), bf16)],
        layer_input, rate_weight, token_keys, token_values,
        name="logits", scalars=(where,),
        in_specs=[
            whole(layer_input.shape),
            whole(rate_weight.shape),
            pl.BlockSpec((WINDOW, width), lambda *_: (tail_at, 0)),
            pl.BlockSpec((WINDOW, width), lambda *_: (tail_at, 0)),
        ],
        flops=2 * rows * features * 128, moved=2 * rows * features,
    )
    distance = 1
    while True:
        got = exchanged(send, "head", distance)
        distance *= 2
        if distance >= head_count:
            break
        both = (keep + got).reshape(-1, 2, SUBLANES, rows)
        bit = (where[1] // distance) % 2
        keep = lax.dynamic_index_in_dim(both, bit, 1, keepdims=False)
        send = lax.dynamic_index_in_dim(both, 1 - bit, 1, keepdims=False)
    keep_logit, got_logit = keep[0], got[0]
    previous = passed_along(tail, "tok")

    backward = []
    for head in range(local_heads):
        tokens = pl.BlockSpec((rows, HDIM), lambda *_, head=head: (0, head))
        weights = pl.BlockSpec((1, HDIM, ffn), lambda *_, head=head: (head, 0, 0))
        weights_down = pl.BlockSpec((1, ffn, HDIM), lambda *_, head=head: (head, 0, 0))
        backward += call(
            backward_kernel,
            [
                struct((rows, 2 * ffn), bf16),
                struct((rows, ffn), bf16),
                struct((HDIM, rows), bf16),
                struct((HDIM, rows), bf16),
            ],
            token_keys, token_values, first_weight, third_weight, second_weight,
            name="backward",
            in_specs=[tokens, tokens, weights, weights, weights_down],
            flops=6 * rows * HDIM * ffn, moved=8 * rows * ffn,
        )
    sums = (chips * HDIM + shared * (HDIM // 2), ffn)
    keep, send = call(
        functools.partial(gradient_kernel, local_heads=local_heads, owners=owners),
        [struct(sums, f32), struct(sums, bf16)],
        keep_logit, got_logit, *backward,
        name="gradients", scalars=(where,),
        flops=2 * matrices * rows * HDIM * ffn, moved=8 * local_heads * rows * ffn,
    )

    got = exchanged(send, "tok", 1)
    piece = (HDIM + shared * part, ffn)
    own, *sends = call(
        functools.partial(chip_sum_kernel, owners=owners, shared=shared),
        [struct(piece, f32)] + [struct(piece, bf16)] * (chips - 1),
        keep, got,
        name="chip_sum", scalars=(where,),
        flops=sums[0] * ffn, moved=8 * sums[0] * ffn,
    )
    addends = [own] + [exchanged(sends[r - 1], "tok", 2 * r) for r in range(1, chips)]
    distance = owners
    while distance < tok_count:
        total = sum(a.astype(f32) for a in addends)
        addends = [total, exchanged(total, "tok", distance)]
        distance *= 2

    tokens = pl.BlockSpec((rows, HDIM), lambda head, *_: (0, head))
    (attended,) = call(
        attention_kernel,
        [struct((rows, width), f32)],
        token_queries, token_keys, token_values, previous, previous,
        name="attention", scalars=(where,), grid=(local_heads,),
        in_specs=[
            tokens, tokens, tokens,
            pl.BlockSpec((WINDOW, HDIM), lambda head, *_: (0, head)),
            pl.BlockSpec((WINDOW, HDIM), lambda head, *_: (1, head)),
        ],
        out_specs=[tokens],
        flops=8 * rows * width * WINDOW, moved=12 * rows * width,
    )

    own_head = lambda *a: ((a[-1][0] % owners) // KINDS, 0, 0)
    own_weight, shared_weight = call(
        functools.partial(weight_kernel, owners=owners),
        [struct((HDIM, ffn), f32)] * 2,
        first_weight, third_weight, second_weight, second_weight,
        name="weights", scalars=(where,),
        in_specs=[
            pl.BlockSpec((1, HDIM, ffn), own_head),
            pl.BlockSpec((1, HDIM, ffn), own_head),
            pl.BlockSpec((1, ffn, HDIM), own_head),
            pl.BlockSpec((1, ffn, HDIM), lambda *_: (local_heads - 1, 0, 0)),
        ],
        flops=0, moved=24 * HDIM * ffn,
    )
    (updated,) = call(
        functools.partial(update_kernel, owners=owners),
        [struct(piece, bf16)],
        own_weight, *addends,
        name="update", scalars=(where, update_scale),
        flops=STEPS * 10 * HDIM * HDIM * ffn // 2, moved=16 * HDIM * ffn,
    )
    near = [updated] + [exchanged(updated, "tok", 2 * r) for r in range(1, chips)]
    far = [exchanged(block, "tok", 1) for block in near]

    (mixed,) = call(
        functools.partial(apply_kernel, local_heads=local_heads, owners=owners, shared=shared),
        [struct((rows, width), bf16)],
        token_queries, attended, out_gain.reshape(1, width), shared_weight, *near, *far,
        name="apply", scalars=(where, update_scale),
        scratch=[
            pltpu.VMEM((matrices, HDIM, ffn), bf16),
            pltpu.VMEM((shared, HDIM, ffn), bf16),
        ],
        flops=2 * matrices * rows * HDIM * ffn, moved=8 * rows * width,
    )
    return mixed


def solution(mesh):
    placed = (
        P("tok", "head"),
        P("head", None),
        P("tok", "head"),
        P("tok", "head"),
        P("tok", "head"),
        P("head", None, None),
        P("head", None, None),
        P("head", None, None),
        P("head"),
        P("head"),
    )
    return jax.shard_map(
        on_device, mesh=mesh, in_specs=placed, out_specs=P("tok", "head"), check_vma=False
    )
```
